256 devices in a mesh: ctx: 128 (over x, z, y_lo, core), head: 2 (over y_hi).
Axes of the slice: x: 4, y: 4 (y_hi: 2, y_lo: 2; y = y_hi * 2 + y_lo), z: 8, core: 2. Of those that a mesh axis runs over, the one named last changes fastest.
Arguments:
- queries: bfloat16 [32768, 512], P('ctx', 'head'), parts along dimension 1, may hold values from -32 to 32
- keys: bfloat16 [32768, 256], P('ctx', 'head'), parts along dimension 1, may hold values from -16 to 16
- values: bfloat16 [32768, 256], P('ctx', 'head'), parts along dimension 1, may hold values from -6 to 6
- doc_starts: int32 [6], P('head'), parts along dimension 0, may hold values from 1 to 12288, as said below
Outputs:
- attended: bfloat16 [32768, 512], P('ctx', 'head'), parts along dimension 1
The draws below stay inside these ranges and needn't reach their ends.
There are 2 independent parts, one for each index of `head`. The reference program is written for one: setup_inputs(seed, part) draws one part's arguments, and reference() takes and returns one part's arrays. A program takes and returns all parts, laid end to end along the dimension named above; each array names one. Nothing has to cross between parts.
Inputs may be any that keep to these rules, and one draw needn't show every extreme that they name: `doc_starts`: strictly rising; the fourth document starts at exactly 12288.
All inputs are finite; a program needn't handle non-finite values.
Results may differ from the reference program's by a relative error of at most 0.01.
Values may be sent and summed in bfloat16 or wider, within the bound.
A program may use at most 64 MiB of HBM per device.

```python
import jax
import jax.numpy as jnp
from jax import lax

D_HEAD = 128
Q_HEADS = 2
TOKENS = 32768


def draw_shared(key):
    mixed = jax.random.fold_in(key, 17)
    key_query, key_keys, key_docs = jax.random.split(mixed, 3)
    eighth = TOKENS // 8
    first_start = jax.random.randint(jax.random.fold_in(key_docs, 1), (1,), 1, eighth + 1)
    second_start = jax.random.randint(jax.random.fold_in(key_docs, 2), (1,), eighth + 1, 2 * eighth + 1)
    last_start = jnp.full((1,), 3 * eighth, jnp.int32)
    doc_starts = jnp.concatenate([first_start, second_start, last_start]).astype(jnp.int32)
    keys = jnp.clip(4.0 * jax.random.normal(key_keys, (TOKENS, D_HEAD), jnp.float32), -16.0, 16.0)
    queries = jnp.clip(jax.random.normal(key_query, (TOKENS, Q_HEADS * D_HEAD), jnp.float32), -6.0, 6.0)
    return (queries, keys, doc_starts)


def draw_queries(key, part):
    return draw_shared(key)[0].astype(jnp.bfloat16)


def draw_keys(key, part):
    return draw_shared(key)[1].astype(jnp.bfloat16)


def draw_doc_starts(key, part):
    return draw_shared(key)[2]


def block_scale(key, dims, shards, smallest, high):
    gain, own = 1.0, jax.random.fold_in(key, 6)
    for position, parts in shards:
        draws = jnp.exp(jax.random.uniform(jax.random.fold_in(own, position), (parts,), jnp.float32, smallest / len(shards), high / len(shards)))
        gain = gain * jnp.repeat(draws, dims[position] // parts).reshape([-1 if axis == position else 1 for axis in range(len(dims))])
    return gain


def noise(key, dims, deviation, bound, cuts=(), kind=jnp.bfloat16):
    entries = jax.random.normal(key, dims, jnp.float32) * deviation
    if len(cuts) > 0:
        entries = block_scale(key, dims, cuts, -0.22, 0.18) * entries
    return jnp.clip(entries, min=-bound, max=bound).astype(kind)


def setup_inputs(seed: int = 0, part: int = 0) -> dict:
    key_list = jax.random.split(jax.random.key(seed), 5)
    part_splits = jax.random.split(jax.random.fold_in(key_list[4], part), 5)
    return {
        "queries": draw_queries(jax.random.fold_in(jax.random.fold_in(key_list[4], part), 71), part),
        "keys": draw_keys(jax.random.fold_in(jax.random.fold_in(key_list[4], part), 71), part),
        "values": noise(part_splits[2], (TOKENS, D_HEAD), 1.0, 6.0, ((0, 128),)),
        "doc_starts": draw_doc_starts(jax.random.fold_in(jax.random.fold_in(key_list[4], part), 71), part),
    }


SCALE = 144.0 ** -0.5
NEGATIVE = -1.0e30


def doc_index(positions, doc_starts):
    return jnp.sum((positions[:, None] >= doc_starts[None, :]).astype(jnp.int32), axis=1)


def reference(queries, keys, values, doc_starts):
    total_rows = queries.shape[0]
    block_rows = min(512, total_rows)
    key_pos = jnp.arange(total_rows, dtype=jnp.int32)
    key_doc = doc_index(key_pos, doc_starts)
    keys_wide = keys.astype(jnp.float32)
    values_wide = values.astype(jnp.float32)

    def one_block(block_number):
        first_row = block_number * block_rows
        rows = lax.dynamic_slice_in_dim(queries, first_row, block_rows, 0).astype(jnp.float32)
        rows = rows.reshape(block_rows, Q_HEADS, D_HEAD)
        query_pos = first_row + jnp.arange(block_rows, dtype=jnp.int32)
        query_doc = doc_index(query_pos, doc_starts)
        scores = jnp.einsum("qhd,kd->hqk", rows, keys_wide) * SCALE
        visible = (key_pos[None, :] <= query_pos[:, None]) & (key_doc[None, :] == query_doc[:, None])
        scores = jnp.where(visible[None], scores, NEGATIVE)
        row_max = jnp.max(scores, axis=2, keepdims=True)
        expo = jnp.where(visible[None], jnp.exp(scores - row_max), 0.0)
        row_total = jnp.sum(expo, axis=2)
        rounded = expo.astype(jnp.bfloat16).astype(jnp.float32)
        weighted = jnp.einsum("hqk,kd->qhd", rounded, values_wide)
        result = weighted / jnp.transpose(row_total)[:, :, None]
        return result.reshape(block_rows, Q_HEADS * D_HEAD).astype(jnp.bfloat16)

    blocks = lax.map(one_block, jnp.arange(total_rows // block_rows, dtype=jnp.int32))
    return blocks.reshape(total_rows, Q_HEADS * D_HEAD)
```

```python
import functools
import math

import jax
import jax.numpy as jnp
from jax import lax
from jax.experimental import pallas as pl
from jax.experimental.pallas import tpu as pltpu
from jax.sharding import PartitionSpec as P

D = 128
H = 2
NX, NZ, NY, NC = 4, 8, 2, 2
PLANE = NZ * NY * NC
EDGE = 48
NEG = -1e30
C2 = math.log2(math.e) / 12.0
SENDS = 31


def ctx_of(x, z, y, c):
    return ((x * NZ + z) * NY + y) * NC + c


def kernel(
    docs, q_in, k_in, v_in, out,
    qbuf, kbuf, vbuf, acc, mx, tot, osend, ssend, orecv, srecv,
    ksem, vsem, qsem, osem, rsem, ksent, vsent, qsent, osent, rsent,
):
    sh = k_in.shape[0]
    grp = NY * NC * sh
    me = lax.axis_index("ctx")
    x = me // PLANE
    z = (me // (NY * NC)) % NZ
    y = (me // NC) % NY
    c = me % NC
    up = ctx_of(x, (z + 1) % NZ, y, c)
    down = ctx_of(x, (z + NZ - 1) % NZ, y, c)
    across = ctx_of(x, z, 1 - y, c)
    twin = ctx_of(x, z, y, 1 - c)

    def shard(zz, yy, cc):
        return (zz * NY + yy) * NC + cc

    def rows(j):
        return pl.ds(pl.multiple_of(j * sh, sh), sh)

    def send(src, dst, sent, got, to):
        return pltpu.make_async_remote_copy(
            src_ref=src, dst_ref=dst, send_sem=sent, recv_sem=got,
            device_id={"ctx": to}, device_id_type=pl.DeviceIdType.MESH,
        )

    def k_send(j, to, src=None):
        send(kbuf.at[rows(j)] if src is None else src, kbuf.at[rows(j)], ksent, ksem.at[j], to).start()

    def v_send(j, to, src=None):
        send(vbuf.at[rows(j)] if src is None else src, vbuf.at[rows(j)], vsent, vsem.at[j], to).start()

    def k_wait(j):
        send(kbuf.at[rows(j)], kbuf.at[rows(j)], ksent, ksem.at[j], twin).wait_recv()

    def v_wait(j):
        send(vbuf.at[rows(j)], vbuf.at[rows(j)], vsent, vsem.at[j], twin).wait_recv()

    mine = shard(z, y, c)
    own = [
        pltpu.make_async_copy(q_in, qbuf.at[0], qsem.at[0]),
        pltpu.make_async_copy(k_in, kbuf.at[rows(mine)], ksem.at[mine]),
        pltpu.make_async_copy(v_in, vbuf.at[rows(mine)], vsem.at[mine]),
    ]
    for copy in own:
        copy.start()

    low = z < NZ // 2
    host = {1: (x == 2) | (x == 1) | ((x == 0) & low), 2: x == 1}
    guest = {1: (x == 3) | (x == 2) | ((x == 1) & low), 2: x == 3}

    barrier = pltpu.get_barrier_semaphore()
    partners = [up, down, across, twin]
    partners += [ctx_of((x + step) % NX, z, y, c) for step in (1, 2, 3)]
    for partner in partners:
        pl.semaphore_signal(barrier, inc=1, device_id={"ctx": partner}, device_id_type=pl.DeviceIdType.MESH)

    for slot in range(3):
        for h in range(H):
            mx[slot, h] = jnp.full((sh, D), NEG, jnp.float32)
            tot[slot, h] = jnp.zeros((sh, D), jnp.float32)
            acc[slot, h] = jnp.zeros((sh, D), jnp.float32)

    pl.semaphore_wait(barrier, len(partners))

    k_send(mine, up, k_in)
    k_send(mine, down, k_in)
    k_send(mine, across, k_in)
    v_send(mine, across, v_in)
    for slot in (1, 2):
        @pl.when(guest[slot])
        def _(slot=slot):
            send(q_in, qbuf.at[slot], qsent.at[slot], qsem.at[slot], ctx_of((x + NX - slot) % NX, z, y, c)).start()
    v_send(mine, up, v_in)
    v_send(mine, down, v_in)
    k_send(mine, twin, k_in)
    v_send(mine, twin, v_in)

    cross = shard(z, 1 - y, c)
    v_wait(cross)
    v_send(cross, up)
    v_send(cross, down)
    v_send(cross, twin)
    k_wait(cross)
    k_send(cross, twin)
    for copy in own:
        copy.wait()
    for slot in (1, 2):
        @pl.when(host[slot])
        def _(slot=slot):
            send(q_in, qbuf.at[slot], qsent.at[slot], qsem.at[slot], twin).wait_recv()

    def attend(slot, g, masked):
        k = kbuf[pl.ds(pl.multiple_of(g * grp, grp), grp), :]
        v = vbuf[pl.ds(pl.multiple_of(g * grp, grp), grp), :]
        vv = jnp.concatenate([v, jnp.ones_like(v)], axis=1)
        if masked:
            q0 = ctx_of(x + slot, z, y, c) * sh
            k0 = (x * PLANE + g * NY * NC) * sh
            qpos = q0 + lax.broadcasted_iota(jnp.int32, (sh, D), 0)
            lo = jnp.zeros((sh, D), jnp.int32)
            for i in range(3):
                lo = jnp.where(qpos >= docs[i], docs[i], lo)
            lane = lax.broadcasted_iota(jnp.int32, (sh, D), 1)
        for h in range(H):
            q = qbuf[slot, :, h * D:(h + 1) * D]
            s = lax.dot_general(q, k, (((1,), (1,)), ((), ())), preferred_element_type=jnp.float32)
            parts = [s[:, j * D:(j + 1) * D] for j in range(grp // D)]
            if masked:
                parts = [
                    jnp.where((lane + (k0 + j * D) <= qpos) & (lane + (k0 + j * D) >= lo), part, NEG)
                    for j, part in enumerate(parts)
                ]
            top = functools.reduce(jnp.maximum, parts)
            old = mx[slot, h]
            new = jnp.maximum(old, jnp.max(top, axis=1, keepdims=True))
            new2 = new * C2
            p = jnp.concatenate([jnp.exp2(part * C2 - new2).astype(jnp.bfloat16) for part in parts], axis=1)
            decay = jnp.exp2(old * C2 - new2)
            pv = jnp.dot(p, vv, preferred_element_type=jnp.float32)
            mx[slot, h] = new
            tot[slot, h] = tot[slot, h] * decay + pv[:, D:]
            acc[slot, h] = acc[slot, h] * decay + pv[:, :D]

    def task(slot, g):
        if_own = (slot == 0) & (g <= z) & jnp.logical_not((x == 1) & (z >= NZ // 2) & (g < NZ // 2))
        if_one = (slot == 1) & ((x == 2) | ((x == 1) & (g >= NZ // 2)) | ((x == 0) & low))
        if_two = (slot == 2) & (x == 1) & (g >= NZ // 2)
        needed = if_own | if_one | if_two
        masked = ((slot == 0) & (g == z)) | (x == 0) | ((slot == 0) & (x == 1) & low)

        @pl.when(needed & masked)
        def _():
            attend(slot, g, True)

        @pl.when(needed & jnp.logical_not(masked))
        def _():
            attend(slot, g, False)

    eye = lax.broadcasted_iota(jnp.int32, (D, D), 0) == lax.broadcasted_iota(jnp.int32, (D, D), 1)

    def finish(slot):
        for h in range(H):
            weight = tot[slot, h]
            osend[slot - 1, :, h * D:(h + 1) * D] = (acc[slot, h] / weight).astype(jnp.bfloat16)
            lse = mx[slot, h] * C2 + jnp.log2(weight)
            for b in range(sh // D):
                block = jnp.where(eye, lse[b * D:(b + 1) * D], 0.0)
                ssend[slot - 1, pl.ds(h * (sh // D) + b, 1), :] = jnp.sum(block, axis=0, keepdims=True)

    def o_copies(slot):
        to = ctx_of((x + slot) % NX, z, y, c)
        i = slot - 1
        return (
            send(osend.at[i], orecv.at[i], osent.at[i], osem.at[i], to),
            send(ssend.at[i], srecv.at[i], rsent.at[i], rsem.at[i], to),
        )

    @pl.loop(1, NZ // 2 + 2)
    def _(s):
        up_z = (z + NZ - s) % NZ
        down_z = (z + s) % NZ

        @pl.when(s <= NZ // 2)
        def _():
            j = shard(up_z, y, c)
            k_wait(j)

            @pl.when(s < NZ // 2)
            def _():
                k_send(j, up)
            k_send(j, across)
            k_send(j, twin)

        @pl.when(s < NZ // 2)
        def _():
            j = shard(down_z, y, c)
            k_wait(j)

            @pl.when(s < NZ // 2 - 1)
            def _():
                k_send(j, down)
            k_send(j, across)
            k_send(j, twin)

        for side in (y, 1 - y):
            @pl.when(s < NZ // 2)
            def _(side=side):
                j = shard(up_z, side, c)
                v_wait(j)

                @pl.when(s < NZ // 2 - 1)
                def _():
                    v_send(j, up)
                v_send(j, twin)

            @pl.when(s <= NZ // 2)
            def _(side=side):
                j = shard(down_z, side, c)
                v_wait(j)

                @pl.when(s < NZ // 2)
                def _():
                    v_send(j, down)
                v_send(j, twin)

        r = s - 1
        first = (z + NZ - r) % NZ
        second = (z + r) % NZ

        @pl.when(r > 0)
        def _():
            j = shard(first, 1 - y, c)
            k_wait(j)
            k_send(j, twin)

        @pl.when((r > 0) & (r < NZ // 2))
        def _():
            j = shard(second, 1 - y, c)
            k_wait(j)
            k_send(j, twin)

        def group(g, final):
            for yy in range(NY):
                k_wait(shard(g, yy, 1 - c))
                v_wait(shard(g, yy, 1 - c))

            @pl.loop(0, 2)
            def _(i):
                task(2 - i, g)

            if final:
                for slot in (1, 2):
                    @pl.when((r == NZ // 2) & host[slot])
                    def _(slot=slot):
                        finish(slot)
                        for copy in o_copies(slot):
                            copy.start()
            task(0, g)

        sides = 2 - ((r == 0) | (r == NZ // 2)).astype(jnp.int32)

        @pl.loop(0, sides)
        def _(i):
            g = first * (1 - i) + second * i
            group(g, True)

    for slot in (1, 2):
        @pl.when(guest[slot])
        def _(slot=slot):
            for copy in o_copies(slot):
                copy.wait_recv()
            send(q_in, qbuf.at[slot], qsent.at[slot], qsem.at[slot], twin).wait_send()

    def merge(slots):
        for h in range(H):
            for b in range(sh // D):
                here = slice(b * D, (b + 1) * D)
                m2 = mx[0, h, here] * C2
                best = m2
                lses = []
                for slot in slots:
                    row = srecv[slot - 1, pl.ds(h * (sh // D) + b, 1), :]
                    col = jnp.sum(jnp.where(eye, row, 0.0), axis=1, keepdims=True)
                    lse = jnp.broadcast_to(col, (D, D))
                    lses.append(lse)
                    best = jnp.maximum(best, lse)
                w = jnp.exp2(m2 - best)
                num = acc[0, h, here] * w
                den = tot[0, h, here] * w
                for slot, lse in zip(slots, lses):
                    w = jnp.exp2(lse - best)
                    num += orecv[slot - 1, here, h * D:(h + 1) * D].astype(jnp.float32) * w
                    den += w
                out[here, h * D:(h + 1) * D] = (num / den).astype(out.dtype)

    @pl.when(guest[2])
    def _():
        merge((1, 2))

    @pl.when(guest[1] & jnp.logical_not(guest[2]))
    def _():
        merge((1,))

    @pl.when(jnp.logical_not(guest[1]))
    def _():
        merge(())

    for slot in (1, 2):
        @pl.when(host[slot])
        def _(slot=slot):
            for copy in o_copies(slot):
                copy.wait_send()
    send(kbuf.at[pl.ds(0, SENDS * sh)], kbuf.at[pl.ds(0, SENDS * sh)], ksent, ksem.at[0], twin).wait_send()
    send(vbuf.at[pl.ds(0, SENDS * sh)], vbuf.at[pl.ds(0, SENDS * sh)], vsent, vsem.at[0], twin).wait_send()


def shards(queries, keys, values, doc_starts):
    sh = keys.shape[0]
    any_spec = pl.BlockSpec(memory_space=pl.ANY)
    dma = pltpu.SemaphoreType.DMA
    return pl.pallas_call(
        kernel,
        out_shape=jax.ShapeDtypeStruct((sh, H * D), jnp.bfloat16),
        in_specs=[pl.BlockSpec(memory_space=pltpu.SMEM), any_spec, any_spec, any_spec],
        out_specs=pl.BlockSpec(memory_space=pltpu.VMEM),
        scratch_shapes=[
            pltpu.VMEM((3, sh, H * D), jnp.bfloat16),
            pltpu.VMEM((PLANE * sh, D), jnp.bfloat16),
            pltpu.VMEM((PLANE * sh, D), jnp.bfloat16),
            pltpu.VMEM((3, H, sh, D), jnp.float32),
            pltpu.VMEM((3, H, sh, D), jnp.float32),
            pltpu.VMEM((3, H, sh, D), jnp.float32),
            pltpu.VMEM((2, sh, H * D), jnp.bfloat16),
            pltpu.VMEM((2, H * sh // D, D), jnp.float32),
            pltpu.VMEM((2, sh, H * D), jnp.bfloat16),
            pltpu.VMEM((2, H * sh // D, D), jnp.float32),
            dma((PLANE,)), dma((PLANE,)), dma((3,)), dma((2,)), dma((2,)),
            dma, dma, dma((3,)), dma((2,)), dma((2,)),
        ],
        compiler_params=pltpu.CompilerParams(collective_id=0, has_side_effects=True),
        name="plane_attention",
    )(doc_starts, queries, keys, values)


def solution(mesh):
    in_specs = (P("ctx", "head"), P("ctx", "head"), P("ctx", "head"), P("head"))
    out_specs = P("ctx", "head")
    return jax.shard_map(shards, mesh=mesh, in_specs=in_specs, out_specs=out_specs, check_vma=False)
```

```python
import functools
import math

import jax
import jax.numpy as jnp
from jax import lax
from jax.experimental import pallas as pl
from jax.experimental.pallas import tpu as pltpu
from jax.sharding import PartitionSpec as P

D = 128
H = 2
NX, NZ, NY, NC = 4, 8, 2, 2
PLANE = NZ * NY * NC
SLOTS = 6
ROWS = 256
BEGIN = (7, 5, 1, 2, 3, 4)
CUT = 2
NEG = -1e30
C2 = math.log2(math.e) / 12.0
SENDS = 26


def ctx_of(x, z, y, c):
    return ((x * NZ + z) * NY + y) * NC + c


def kernel(
    docs, q_in, k_in, v_in, out,
    qbuf, kv, acc, mx, tot, osend, ssend, orecv, srecv,
    kvsem, qsem, osem, rsem, kvsent, first_sent, qsent, osent, rsent,
):
    sh = k_in.shape[0]
    grp = NC * sh
    half = NZ // 2
    piece = sh // CUT
    pieces = 2 * CUT
    vbase = NZ * NC
    me = lax.axis_index("ctx")
    x = me // PLANE
    z = (me // (NY * NC)) % NZ
    y = (me // NC) % NY
    c = me % NC
    up = ctx_of(x, (z + 1) % NZ, y, c)
    down = ctx_of(x, (z + NZ - 1) % NZ, y, c)
    twin = ctx_of(x, z, y, 1 - c)

    def shard(zz, cc):
        return zz * NC + cc

    def rows(j, ch):
        start = (ch // CUT * vbase + j) * sh + ch % CUT * piece
        return pl.ds(pl.multiple_of(start, piece), piece)

    def send(src, dst, sent, got, to):
        return pltpu.make_async_remote_copy(
            src_ref=src, dst_ref=dst, send_sem=sent, recv_sem=got,
            device_id={"ctx": to}, device_id_type=pl.DeviceIdType.MESH,
        )

    def kv_send(j, ch, to):
        send(kv.at[rows(j, ch)], kv.at[rows(j, ch)], kvsent, kvsem.at[j * pieces + ch], to).start()

    def kv_wait(j, ch):
        send(kv.at[rows(j, ch)], kv.at[rows(j, ch)], kvsent, kvsem.at[j * pieces + ch], twin).wait_recv()

    mine = shard(z, c)
    own = [pltpu.make_async_copy(q_in, qbuf.at[0], qsem.at[0])]
    for ch in range(pieces):
        src = (k_in, v_in)[ch // CUT].at[pl.ds(ch % CUT * piece, piece)]
        own.append(pltpu.make_async_copy(src, kv.at[rows(mine, ch)], kvsem.at[mine * pieces + ch]))
    for copy in own:
        copy.start()

    low = z < half
    host = (x >= 0, (x == 2) | (x == 1) | ((x == 0) & low), x == 1)
    guest = (x >= 0, (x == 3) | (x == 2) | ((x == 1) & low), x == 3)

    def hosted(slot):
        sx = slot // 2
        return (sx == 0) | ((sx == 1) & host[1]) | ((sx == 2) & host[2])

    def home(slot):
        side = y + (slot % 2) * (1 - 2 * y)
        return ctx_of((x + slot // 2) % NX, z, side, c)

    def q_copy(slot):
        side = y + (slot % 2) * (1 - 2 * y)
        to = ctx_of((x + NX - slot // 2) % NX, z, side, c)
        return send(q_in, qbuf.at[slot], qsent.at[slot], qsem.at[slot], to)

    barrier = pltpu.get_barrier_semaphore()
    partners = [up, down, twin]
    partners += [ctx_of((x + dx) % NX, z, side, c) for dx in range(NX) for side in (y, 1 - y)][1:]
    for partner in partners:
        pl.semaphore_signal(barrier, inc=1, device_id={"ctx": partner}, device_id_type=pl.DeviceIdType.MESH)

    pl.semaphore_wait(barrier, len(partners))

    def first(ch, i):
        src = (k_in, v_in)[ch // CUT].at[pl.ds(ch % CUT * piece, piece)]
        return send(src, kv.at[rows(mine, ch)], first_sent.at[2 * ch + i], kvsem.at[mine * pieces + ch], (up, down)[i])

    for ch in range(pieces):
        for i in range(2):
            first(ch, i).start()
    for slot in (2, 1, 3, 4, 5):
        @pl.when(guest[slot // 2])
        def _(slot=slot):
            q_copy(slot).start()
    for copy in own:
        copy.wait()
    for ch in range(pieces):
        kv_send(mine, ch, twin)

    @pl.loop(0, SLOTS)
    def _(slot):
        for h in range(H):
            mx[slot, h] = jnp.full((sh, D), NEG, jnp.float32)
            tot[slot, h] = jnp.zeros((sh, D), jnp.float32)
            acc[slot, h] = jnp.zeros((sh, D), jnp.float32)

    def group(n):
        d = (n + 1) // 2
        back = n % 2
        return (z + back * (NZ - d) + (1 - back) * d) % NZ

    def attend(slot, g, masked):
        k = kv[pl.ds(pl.multiple_of(g * grp, grp), grp), :]
        v = kv[pl.ds(pl.multiple_of(vbase * sh + g * grp, grp), grp), :]
        if masked:
            q0 = home(slot) * sh
            k0 = ctx_of(x, g, y, 0) * sh
            qpos = q0 + lax.broadcasted_iota(jnp.int32, (sh, D), 0)
            lo = jnp.zeros((sh, D), jnp.int32)
            for i in range(3):
                lo = jnp.where(qpos >= docs[i], docs[i], lo)
            lane = lax.broadcasted_iota(jnp.int32, (sh, D), 1)
        def scores(h, b):
            q = qbuf[slot, b * ROWS:(b + 1) * ROWS, h * D:(h + 1) * D]
            return lax.dot_general(q, k, (((1,), (1,)), ((), ())), preferred_element_type=jnp.float32)

        def mask(s, b):
            parts = [s[:, j * D:(j + 1) * D] for j in range(grp // D)]
            if masked:
                here = slice(b * ROWS, (b + 1) * ROWS)
                parts = [
                    jnp.where(
                        (lane[here] + (k0 + j * D) <= qpos[here]) & (lane[here] + (k0 + j * D) >= lo[here]), part, NEG
                    )
                    for j, part in enumerate(parts)
                ]
            return parts

        def soft(s, h, b):
            here = slice(b * ROWS, (b + 1) * ROWS)
            parts = mask(s, b)
            top = functools.reduce(jnp.maximum, parts)
            old = mx[slot, h, here]
            new = jnp.maximum(old, jnp.max(top, axis=1, keepdims=True))
            mx[slot, h, here] = new
            new2 = new * C2
            parts = [jnp.exp2(part * C2 - new2) for part in parts]
            p = jnp.concatenate([part.astype(jnp.bfloat16) for part in parts], axis=1)
            decay = jnp.exp2(old * C2 - new2)
            tot[slot, h, here] = tot[slot, h, here] * decay + functools.reduce(jnp.add, parts)
            return p, decay

        def gather(p, decay, h, b):
            here = slice(b * ROWS, (b + 1) * ROWS)
            pv = jnp.dot(p, v, preferred_element_type=jnp.float32)
            acc[slot, h, here] = acc[slot, h, here] * decay + pv

        todo = [(h, b) for h in range(H) for b in range(sh // ROWS)]
        s = scores(*todo[0])
        for at, (h, b) in enumerate(todo):
            ahead = scores(*todo[at + 1]) if at + 1 < len(todo) else None
            p, decay = soft(s, h, b)
            gather(p, decay, h, b)
            s = ahead

    def task(slot, g):
        sx = slot // 2
        if_own = (sx == 0) & (g <= z) & jnp.logical_not((x == 1) & (z >= half) & (g < half))
        if_one = (sx == 1) & ((x == 2) | ((x == 1) & (g >= half)) | ((x == 0) & low))
        if_two = (sx == 2) & (x == 1) & (g >= half)
        needed = if_own | if_one | if_two
        masked = ((sx == 0) & (g == z)) | (x == 0) | ((sx == 0) & (x == 1) & low)

        @pl.when(needed & masked)
        def _():
            attend(slot, g, True)

        @pl.when(needed & jnp.logical_not(masked))
        def _():
            attend(slot, g, False)

    eye = lax.broadcasted_iota(jnp.int32, (D, D), 0) == lax.broadcasted_iota(jnp.int32, (D, D), 1)

    def finish(slot):
        for h in range(H):
            weight = jnp.broadcast_to(jnp.sum(tot[slot, h], axis=1, keepdims=True), (sh, D))
            osend[slot - 1, :, h * D:(h + 1) * D] = (acc[slot, h] / weight).astype(jnp.bfloat16)
            lse = mx[slot, h] * C2 + jnp.log2(weight)
            for b in range(sh // D):
                block = jnp.where(eye, lse[b * D:(b + 1) * D], 0.0)
                ssend[slot - 1, pl.ds(h * (sh // D) + b, 1), :] = jnp.sum(block, axis=0, keepdims=True)

    def o_copies(slot):
        to = home(slot)
        i = slot - 1
        return (
            send(osend.at[i], orecv.at[i], osent.at[i], osem.at[i], to),
            send(ssend.at[i], srecv.at[i], rsent.at[i], rsem.at[i], to),
        )

    @pl.loop(1, half + 2)
    def _(s):
        up_j = shard((z + NZ - s) % NZ, c)
        down_j = shard((z + s) % NZ, c)

        @pl.loop(0, pieces)
        def _(ch):
            late = ch // CUT
            last_up = half - late
            last_down = half - 1 + late

            @pl.when(s <= last_up)
            def _():
                kv_wait(up_j, ch)

                @pl.when(s < last_up)
                def _():
                    kv_send(up_j, ch, up)

            @pl.when(s <= last_down)
            def _():
                kv_wait(down_j, ch)

                @pl.when(s < last_down)
                def _():
                    kv_send(down_j, ch, down)

            @pl.when(s <= last_up)
            def _():
                kv_send(up_j, ch, twin)

            @pl.when(s <= last_down)
            def _():
                kv_send(down_j, ch, twin)

            n = 2 * s - 3 + ch // CUT

            @pl.when((n >= 0) & (n < NZ))
            def _():
                @pl.when(ch % CUT == 0)
                def _():
                    for part in range(pieces):
                        kv_wait(shard(group(n), 1 - c), part)

                @pl.loop(0, SLOTS // CUT)
                def _(t):
                    last = (n == NZ - 1).astype(jnp.int32)
                    slot = SLOTS - 1 - last * (3 * (ch % CUT) + t) - (1 - last) * (ch % CUT + 2 * t)
                    begin = jnp.array(BEGIN[0], jnp.int32)
                    for at in range(1, SLOTS):
                        begin = jnp.where(slot == at, BEGIN[at], begin)

                    @pl.when(hosted(slot) & (n >= begin))
                    def _():
                        @pl.when((slot > 0) & (n == begin))
                        def _():
                            q_copy(slot).wait_recv()

                        start = n * (n > begin).astype(jnp.int32)

                        @pl.loop(start, n + 1)
                        def _(k):
                            task(slot, group(k))

                        @pl.when((n == NZ - 1) & (slot > 0))
                        def _():
                            finish(slot)
                            for copy in o_copies(slot):
                                copy.start()

    def fold(slot):
        for copy in o_copies(slot):
            copy.wait_recv()
        for h in range(H):
            for b in range(sh // D):
                here = slice(b * D, (b + 1) * D)
                row = srecv[slot - 1, pl.ds(h * (sh // D) + b, 1), :]
                lse = jnp.broadcast_to(jnp.sum(jnp.where(eye, row, 0.0), axis=1, keepdims=True), (D, D))
                m2 = mx[0, h, here]
                best = jnp.maximum(m2, lse)
                keep = jnp.exp2(m2 - best)
                w = jnp.exp2(lse - best)
                part = orecv[slot - 1, here, h * D:(h + 1) * D].astype(jnp.float32)
                acc[0, h, here] = acc[0, h, here] * keep + part * w
                tot[0, h, here] = tot[0, h, here] * keep + w
                mx[0, h, here] = best

    for h in range(H):
        mx[0, h] = mx[0, h] * C2
        tot[0, h] = jnp.broadcast_to(jnp.sum(tot[0, h], axis=1, keepdims=True), (sh, D))

    fold(1)

    @pl.loop(0, SLOTS - 2)
    def _(t):
        slot = 2 + (t + 2) % 4

        @pl.when(((slot < 4) & guest[1]) | ((slot >= 4) & guest[2]))
        def _():
            fold(slot)

    for h in range(H):
        out[:, h * D:(h + 1) * D] = (acc[0, h] / tot[0, h]).astype(out.dtype)

    for slot in range(1, SLOTS):
        @pl.when(guest[slot // 2])
        def _(slot=slot):
            q_copy(slot).wait_send()

    for slot in range(1, SLOTS):
        @pl.when(host[slot // 2])
        def _(slot=slot):
            for copy in o_copies(slot):
                copy.wait_send()
    for ch in range(pieces):
        for i in range(2):
            first(ch, i).wait_send()
    send(kv.at[pl.ds(0, SENDS * sh)], kv.at[pl.ds(0, SENDS * sh)], kvsent, kvsem.at[0], twin).wait_send()


def shards(queries, keys, values, doc_starts):
    sh = keys.shape[0]
    any_spec = pl.BlockSpec(memory_space=pl.ANY)
    dma = pltpu.SemaphoreType.DMA
    return pl.pallas_call(
        kernel,
        out_shape=jax.ShapeDtypeStruct((sh, H * D), jnp.bfloat16),
        in_specs=[pl.BlockSpec(memory_space=pltpu.SMEM), any_spec, any_spec, any_spec],
        out_specs=pl.BlockSpec(memory_space=pltpu.VMEM),
        scratch_shapes=[
            pltpu.VMEM((SLOTS, sh, H * D), jnp.bfloat16),
            pltpu.VMEM((2 * NZ * NC * sh, D), jnp.bfloat16),
            pltpu.VMEM((SLOTS, H, sh, D), jnp.float32),
            pltpu.VMEM((SLOTS, H, sh, D), jnp.float32),
            pltpu.VMEM((SLOTS, H, sh, D), jnp.float32),
            pltpu.VMEM((SLOTS - 1, sh, H * D), jnp.bfloat16),
            pltpu.VMEM((SLOTS - 1, H * sh // D, D), jnp.float32),
            pltpu.VMEM((SLOTS - 1, sh, H * D), jnp.bfloat16),
            pltpu.VMEM((SLOTS - 1, H * sh // D, D), jnp.float32),
            dma((2 * CUT * NZ * NC,)), dma((SLOTS,)), dma((SLOTS - 1,)), dma((SLOTS - 1,)),
            dma, dma((4 * CUT,)), dma((SLOTS,)), dma((SLOTS - 1,)), dma((SLOTS - 1,)),
        ],
        compiler_params=pltpu.CompilerParams(collective_id=0, has_side_effects=True),
        name="ring_attention",
    )(doc_starts, queries, keys, values)


def solution(mesh):
    in_specs = (P("ctx", "head"), P("ctx", "head"), P("ctx", "head"), P("head"))
    out_specs = P("ctx", "head")
    return jax.shard_map(shards, mesh=mesh, in_specs=in_specs, out_specs=out_specs, check_vma=False)
```

```python
import functools
import math

import jax
import jax.numpy as jnp
from jax import lax
from jax.experimental import pallas as pl
from jax.experimental.pallas import tpu as pltpu
from jax.sharding import PartitionSpec as P

D = 128
H = 2
NX, NZ, NY, NC = 4, 8, 2, 2
PLANE = NZ * NY * NC
SLOTS = 6
ROWS = 256
BEGIN = (7, 7, 1, 2, 3, 4)
CUT = 1
NEG = -1e30
C2 = math.log2(math.e) / 12.0
SENDS = 26


def ctx_of(x, z, y, c):
    return ((x * NZ + z) * NY + y) * NC + c


def kernel(
    docs, q_in, k_in, v_in, out,
    qbuf, kv, acc, mx, tot, osend, ssend, orecv, srecv,
    kvsem, qsem, osem, rsem, kvsent, first_sent, qsent, osent, rsent,
):
    sh = k_in.shape[0]
    grp = NC * sh
    half = NZ // 2
    piece = sh // CUT
    pieces = 2 * CUT
    vbase = NZ * NC
    me = lax.axis_index("ctx")
    x = me // PLANE
    z = (me // (NY * NC)) % NZ
    y = (me // NC) % NY
    c = me % NC
    up = ctx_of(x, (z + 1) % NZ, y, c)
    down = ctx_of(x, (z + NZ - 1) % NZ, y, c)
    twin = ctx_of(x, z, y, 1 - c)

    def shard(zz, cc):
        return zz * NC + cc

    def rows(j, ch):
        start = (ch // CUT * vbase + j) * sh + ch % CUT * piece
        return pl.ds(pl.multiple_of(start, piece), piece)

    def send(src, dst, sent, got, to):
        return pltpu.make_async_remote_copy(
            src_ref=src, dst_ref=dst, send_sem=sent, recv_sem=got,
            device_id={"ctx": to}, device_id_type=pl.DeviceIdType.MESH,
        )

    def kv_send(j, ch, to):
        send(kv.at[rows(j, ch)], kv.at[rows(j, ch)], kvsent, kvsem.at[j * pieces + ch], to).start()

    def kv_wait(j, ch):
        send(kv.at[rows(j, ch)], kv.at[rows(j, ch)], kvsent, kvsem.at[j * pieces + ch], twin).wait_recv()

    mine = shard(z, c)
    own = [pltpu.make_async_copy(q_in, qbuf.at[0], qsem.at[0])]
    for ch in range(pieces):
        src = (k_in, v_in)[ch // CUT].at[pl.ds(ch % CUT * piece, piece)]
        own.append(pltpu.make_async_copy(src, kv.at[rows(mine, ch)], kvsem.at[mine * pieces + ch]))
    for copy in own:
        copy.start()

    low = z < half
    host = (x >= 0, (x == 2) | (x == 1) | ((x == 0) & low), x == 1)
    guest = (x >= 0, (x == 3) | (x == 2) | ((x == 1) & low), x == 3)

    def hosted(slot):
        sx = slot // 2
        return (sx == 0) | ((sx == 1) & host[1]) | ((sx == 2) & host[2])

    def home(slot):
        side = y + (slot % 2) * (1 - 2 * y)
        return ctx_of((x + slot // 2) % NX, z, side, c)

    def q_copy(slot):
        side = y + (slot % 2) * (1 - 2 * y)
        to = ctx_of((x + NX - slot // 2) % NX, z, side, c)
        return send(q_in, qbuf.at[slot], qsent.at[slot], qsem.at[slot], to)

    barrier = pltpu.get_barrier_semaphore()
    partners = [up, down, twin]
    partners += [ctx_of((x + dx) % NX, z, side, c) for dx in range(NX) for side in (y, 1 - y)][1:]
    for partner in partners:
        pl.semaphore_signal(barrier, inc=1, device_id={"ctx": partner}, device_id_type=pl.DeviceIdType.MESH)

    pl.semaphore_wait(barrier, len(partners))

    def first(ch, i):
        src = (k_in, v_in)[ch // CUT].at[pl.ds(ch % CUT * piece, piece)]
        return send(src, kv.at[rows(mine, ch)], first_sent.at[2 * ch + i], kvsem.at[mine * pieces + ch], (up, down)[i])

    for ch in range(pieces):
        for i in range(2):
            first(ch, i).start()
    for slot in (2, 1, 3, 4, 5):
        @pl.when(guest[slot // 2])
        def _(slot=slot):
            q_copy(slot).start()
    for copy in own:
        copy.wait()
    for ch in range(pieces):
        kv_send(mine, ch, twin)

    @pl.loop(0, SLOTS)
    def _(slot):
        for h in range(H):
            mx[slot, h] = jnp.full((sh, D), NEG, jnp.float32)
            tot[slot, h] = jnp.zeros((sh, D), jnp.float32)
            acc[slot, h] = jnp.zeros((sh, D), jnp.float32)

    def group(n):
        d = (n + 1) // 2
        back = n % 2
        return (z + back * (NZ - d) + (1 - back) * d) % NZ

    def attend(slot, g, masked):
        k = kv[pl.ds(pl.multiple_of(g * grp, grp), grp), :]
        v = kv[pl.ds(pl.multiple_of(vbase * sh + g * grp, grp), grp), :]
        if masked:
            q0 = home(slot) * sh
            k0 = ctx_of(x, g, y, 0) * sh
            qpos = q0 + lax.broadcasted_iota(jnp.int32, (sh, D), 0)
            lo = jnp.zeros((sh, D), jnp.int32)
            for i in range(3):
                lo = jnp.where(qpos >= docs[i], docs[i], lo)
            lane = lax.broadcasted_iota(jnp.int32, (sh, D), 1)
        def scores(h, b):
            q = qbuf[slot, b * ROWS:(b + 1) * ROWS, h * D:(h + 1) * D]
            return lax.dot_general(q, k, (((1,), (1,)), ((), ())), preferred_element_type=jnp.float32)

        def mask(s, b):
            parts = [s[:, j * D:(j + 1) * D] for j in range(grp // D)]
            if masked:
                here = slice(b * ROWS, (b + 1) * ROWS)
                parts = [
                    jnp.where(
                        (lane[here] + (k0 + j * D) <= qpos[here]) & (lane[here] + (k0 + j * D) >= lo[here]), part, NEG
                    )
                    for j, part in enumerate(parts)
                ]
            return parts

        def soft(s, h, b):
            here = slice(b * ROWS, (b + 1) * ROWS)
            parts = mask(s, b)
            top = functools.reduce(jnp.maximum, parts)
            old = mx[slot, h, here]
            new = jnp.maximum(old, jnp.max(top, axis=1, keepdims=True))
            mx[slot, h, here] = new
            new2 = new * C2
            parts = [jnp.exp2(part * C2 - new2) for part in parts]
            p = jnp.concatenate([part.astype(jnp.bfloat16) for part in parts], axis=1)
            decay = jnp.exp2(old * C2 - new2)
            tot[slot, h, here] = tot[slot, h, here] * decay + functools.reduce(jnp.add, parts)
            return p, decay

        def gather(p, decay, h, b):
            here = slice(b * ROWS, (b + 1) * ROWS)
            pv = jnp.dot(p, v, preferred_element_type=jnp.float32)
            acc[slot, h, here] = acc[slot, h, here] * decay + pv

        todo = [(h, b) for h in range(H) for b in range(sh // ROWS)]
        s = scores(*todo[0])
        for at, (h, b) in enumerate(todo):
            ahead = scores(*todo[at + 1]) if at + 1 < len(todo) else None
            p, decay = soft(s, h, b)
            gather(p, decay, h, b)
            s = ahead

    def task(slot, g):
        sx = slot // 2
        if_own = (sx == 0) & (g <= z) & jnp.logical_not((x == 1) & (z >= half) & (g < half))
        if_one = (sx == 1) & ((x == 2) | ((x == 1) & (g >= half)) | ((x == 0) & low))
        if_two = (sx == 2) & (x == 1) & (g >= half)
        needed = if_own | if_one | if_two
        masked = ((sx == 0) & (g == z)) | (x == 0) | ((sx == 0) & (x == 1) & low)

        @pl.when(needed & masked)
        def _():
            attend(slot, g, True)

        @pl.when(needed & jnp.logical_not(masked))
        def _():
            attend(slot, g, False)

    eye = lax.broadcasted_iota(jnp.int32, (D, D), 0) == lax.broadcasted_iota(jnp.int32, (D, D), 1)

    def finish(slot):
        for h in range(H):
            weight = jnp.broadcast_to(jnp.sum(tot[slot, h], axis=1, keepdims=True), (sh, D))
            osend[slot - 1, :, h * D:(h + 1) * D] = (acc[slot, h] / weight).astype(jnp.bfloat16)
            lse = mx[slot, h] * C2 + jnp.log2(weight)
            for b in range(sh // D):
                block = jnp.where(eye, lse[b * D:(b + 1) * D], 0.0)
                ssend[slot - 1, pl.ds(h * (sh // D) + b, 1), :] = jnp.sum(block, axis=0, keepdims=True)

    def o_copies(slot):
        to = home(slot)
        i = slot - 1
        return (
            send(osend.at[i], orecv.at[i], osent.at[i], osem.at[i], to),
            send(ssend.at[i], srecv.at[i], rsent.at[i], rsem.at[i], to),
        )

    @pl.loop(1, half + 2)
    def _(s):
        up_j = shard((z + NZ - s) % NZ, c)
        down_j = shard((z + s) % NZ, c)

        @pl.loop(0, pieces)
        def _(ch):
            late = ch // CUT
            last_up = half - late
            last_down = half - 1 + late

            @pl.when(s <= last_up)
            def _():
                kv_wait(up_j, ch)

                @pl.when(s < last_up)
                def _():
                    kv_send(up_j, ch, up)

            @pl.when(s <= last_down)
            def _():
                kv_wait(down_j, ch)

                @pl.when(s < last_down)
                def _():
                    kv_send(down_j, ch, down)

            @pl.when(s <= last_up)
            def _():
                kv_send(up_j, ch, twin)

            @pl.when(s <= last_down)
            def _():
                kv_send(down_j, ch, twin)

            n = 2 * s - 3 + ch // CUT

            @pl.when((n >= 0) & (n < NZ))
            def _():
                @pl.when(ch % CUT == 0)
                def _():
                    for part in range(pieces):
                        kv_wait(shard(group(n), 1 - c), part)

                @pl.loop(0, SLOTS // CUT)
                def _(t):
                    last = (n == NZ - 1).astype(jnp.int32)
                    slot = SLOTS - 1 - last * (SLOTS // CUT * (ch % CUT) + t) - (1 - last) * (ch % CUT + CUT * t)
                    begin = jnp.array(BEGIN[0], jnp.int32)
                    for at in range(1, SLOTS):
                        begin = jnp.where(slot == at, BEGIN[at], begin)

                    @pl.when(hosted(slot) & (n >= begin))
                    def _():
                        @pl.when((slot > 0) & (n == begin))
                        def _():
                            q_copy(slot).wait_recv()

                        start = n * (n > begin).astype(jnp.int32)

                        @pl.loop(start, n + 1)
                        def _(k):
                            task(slot, group(k))

                        early = ((x == 1) & (z >= half) & (slot > 1)).astype(jnp.int32)

                        @pl.when((n == NZ - 1 - early) & (slot > 0))
                        def _():
                            finish(slot)
                            for copy in o_copies(slot):
                                copy.start()

    def fold(slot):
        for copy in o_copies(slot):
            copy.wait_recv()
        for h in range(H):
            for b in range(sh // D):
                here = slice(b * D, (b + 1) * D)
                row = srecv[slot - 1, pl.ds(h * (sh // D) + b, 1), :]
                lse = jnp.broadcast_to(jnp.sum(jnp.where(eye, row, 0.0), axis=1, keepdims=True), (D, D))
                m2 = mx[0, h, here]
                best = jnp.maximum(m2, lse)
                keep = jnp.exp2(m2 - best)
                w = jnp.exp2(lse - best)
                part = orecv[slot - 1, here, h * D:(h + 1) * D].astype(jnp.float32)
                acc[0, h, here] = acc[0, h, here] * keep + part * w
                tot[0, h, here] = tot[0, h, here] * keep + w
                mx[0, h, here] = best

    for h in range(H):
        mx[0, h] = mx[0, h] * C2
        tot[0, h] = jnp.broadcast_to(jnp.sum(tot[0, h], axis=1, keepdims=True), (sh, D))

    fold(1)

    @pl.loop(0, SLOTS - 2)
    def _(t):
        slot = 2 + (t + 2) % 4

        @pl.when(((slot < 4) & guest[1]) | ((slot >= 4) & guest[2]))
        def _():
            fold(slot)

    for h in range(H):
        out[:, h * D:(h + 1) * D] = (acc[0, h] / tot[0, h]).astype(out.dtype)

    for slot in range(1, SLOTS):
        @pl.when(guest[slot // 2])
        def _(slot=slot):
            q_copy(slot).wait_send()

    for slot in range(1, SLOTS):
        @pl.when(host[slot // 2])
        def _(slot=slot):
            for copy in o_copies(slot):
                copy.wait_send()
    for ch in range(pieces):
        for i in range(2):
            first(ch, i).wait_send()
    send(kv.at[pl.ds(0, SENDS * sh)], kv.at[pl.ds(0, SENDS * sh)], kvsent, kvsem.at[0], twin).wait_send()


def shards(queries, keys, values, doc_starts):
    sh = keys.shape[0]
    any_spec = pl.BlockSpec(memory_space=pl.ANY)
    dma = pltpu.SemaphoreType.DMA
    return pl.pallas_call(
        kernel,
        out_shape=jax.ShapeDtypeStruct((sh, H * D), jnp.bfloat16),
        in_specs=[pl.BlockSpec(memory_space=pltpu.SMEM), any_spec, any_spec, any_spec],
        out_specs=pl.BlockSpec(memory_space=pltpu.VMEM),
        scratch_shapes=[
            pltpu.VMEM((SLOTS, sh, H * D), jnp.bfloat16),
            pltpu.VMEM((2 * NZ * NC * sh, D), jnp.bfloat16),
            pltpu.VMEM((SLOTS, H, sh, D), jnp.float32),
            pltpu.VMEM((SLOTS, H, sh, D), jnp.float32),
            pltpu.VMEM((SLOTS, H, sh, D), jnp.float32),
            pltpu.VMEM((SLOTS - 1, sh, H * D), jnp.bfloat16),
            pltpu.VMEM((SLOTS - 1, H * sh // D, D), jnp.float32),
            pltpu.VMEM((SLOTS - 1, sh, H * D), jnp.bfloat16),
            pltpu.VMEM((SLOTS - 1, H * sh // D, D), jnp.float32),
            dma((2 * CUT * NZ * NC,)), dma((SLOTS,)), dma((SLOTS - 1,)), dma((SLOTS - 1,)),
            dma, dma((4 * CUT,)), dma((SLOTS,)), dma((SLOTS - 1,)), dma((SLOTS - 1,)),
        ],
        compiler_params=pltpu.CompilerParams(collective_id=0, has_side_effects=True),
        name="ring_attention",
    )(doc_starts, queries, keys, values)


def solution(mesh):
    in_specs = (P("ctx", "head"), P("ctx", "head"), P("ctx", "head"), P("head"))
    out_specs = P("ctx", "head")
    return jax.shard_map(shards, mesh=mesh, in_specs=in_specs, out_specs=out_specs, check_vma=False)
```

```python
import functools
import math

import jax
import jax.numpy as jnp
from jax import lax
from jax.experimental import pallas as pl
from jax.experimental.pallas import tpu as pltpu
from jax.sharding import PartitionSpec as P

D = 128
H = 2
NX, NZ, NY, NC = 4, 8, 2, 2
PLANE = NZ * NY * NC
SLOTS = 6
ROWS = 256
BEGIN = (7, 7, 1, 2, 3, 4)
CUT = 1
NEG = -1e30
C2 = math.log2(math.e) / 12.0
SENDS = 26


def ctx_of(x, z, y, c):
    return ((x * NZ + z) * NY + y) * NC + c


def kernel(
    docs, q_in, k_in, v_in, out,
    qbuf, kv, acc, mx, tot, osend, ssend, orecv, srecv,
    kvsem, qsem, osem, rsem, kvsent, first_sent, qsent, osent, rsent,
):
    sh = k_in.shape[0]
    grp = NC * sh
    half = NZ // 2
    piece = sh // CUT
    pieces = 2 * CUT
    vbase = NZ * NC
    me = lax.axis_index("ctx")
    x = me // PLANE
    z = (me // (NY * NC)) % NZ
    y = (me // NC) % NY
    c = me % NC
    up = ctx_of(x, (z + 1) % NZ, y, c)
    down = ctx_of(x, (z + NZ - 1) % NZ, y, c)
    twin = ctx_of(x, z, y, 1 - c)

    def shard(zz, cc):
        return zz * NC + cc

    def rows(j, ch):
        start = (ch // CUT * vbase + j) * sh + ch % CUT * piece
        return pl.ds(pl.multiple_of(start, piece), piece)

    def send(src, dst, sent, got, to):
        return pltpu.make_async_remote_copy(
            src_ref=src, dst_ref=dst, send_sem=sent, recv_sem=got,
            device_id={"ctx": to}, device_id_type=pl.DeviceIdType.MESH,
        )

    def kv_send(j, ch, to):
        send(kv.at[rows(j, ch)], kv.at[rows(j, ch)], kvsent, kvsem.at[j * pieces + ch], to).start()

    def kv_wait(j, ch):
        send(kv.at[rows(j, ch)], kv.at[rows(j, ch)], kvsent, kvsem.at[j * pieces + ch], twin).wait_recv()

    mine = shard(z, c)
    own = [pltpu.make_async_copy(q_in, qbuf.at[0], qsem.at[0])]
    for ch in range(pieces):
        src = (k_in, v_in)[ch // CUT].at[pl.ds(ch % CUT * piece, piece)]
        own.append(pltpu.make_async_copy(src, kv.at[rows(mine, ch)], kvsem.at[mine * pieces + ch]))
    for copy in own:
        copy.start()

    low = z < half
    host = (x >= 0, (x == 2) | (x == 1) | ((x == 0) & low), x == 1)
    guest = (x >= 0, (x == 3) | (x == 2) | ((x == 1) & low), x == 3)

    def hosted(slot):
        sx = slot // 2
        return (sx == 0) | ((sx == 1) & host[1]) | ((sx == 2) & host[2])

    def home(slot):
        side = y + (slot % 2) * (1 - 2 * y)
        return ctx_of((x + slot // 2) % NX, z, side, c)

    def q_copy(slot):
        side = y + (slot % 2) * (1 - 2 * y)
        to = ctx_of((x + NX - slot // 2) % NX, z, side, c)
        return send(q_in, qbuf.at[slot], qsent.at[slot], qsem.at[slot], to)

    barrier = pltpu.get_barrier_semaphore()
    def greet(partner):
        pl.semaphore_signal(barrier, inc=1, device_id={"ctx": partner}, device_id_type=pl.DeviceIdType.MESH)

    for partner in (up, down, twin, ctx_of(x, z, 1 - y, c)):
        greet(partner)
    greeted = jnp.array(4, jnp.int32)
    for dx in range(1, NX):
        other = (x + dx) % NX
        meets = ((x > 0) & (other > 0)) | (low & (x + other == 1))
        greeted += 2 * meets.astype(jnp.int32)

        @pl.when(meets)
        def _(other=other):
            for side in (y, 1 - y):
                greet(ctx_of(other, z, side, c))

    pl.semaphore_wait(barrier, greeted)

    def first(ch, i):
        src = (k_in, v_in)[ch // CUT].at[pl.ds(ch % CUT * piece, piece)]
        return send(src, kv.at[rows(mine, ch)], first_sent.at[2 * ch + i], kvsem.at[mine * pieces + ch], (up, down)[i])

    for ch in range(pieces):
        for i in range(2):
            first(ch, i).start()
    for slot in (2, 1, 3, 4, 5):
        @pl.when(guest[slot // 2])
        def _(slot=slot):
            q_copy(slot).start()
    for ch in range(pieces):
        src = (k_in, v_in)[ch // CUT].at[pl.ds(ch % CUT * piece, piece)]
        send(src, kv.at[rows(mine, ch)], kvsent, kvsem.at[mine * pieces + ch], twin).start()
    for copy in own:
        copy.wait()

    @pl.loop(0, SLOTS)
    def _(slot):
        for h in range(H):
            mx[slot, h] = jnp.full((sh, D), NEG, jnp.float32)
            tot[slot, h] = jnp.zeros((sh, D), jnp.float32)
            acc[slot, h] = jnp.zeros((sh, D), jnp.float32)

    def group(n):
        d = (n + 1) // 2
        back = n % 2
        return (z + back * (NZ - d) + (1 - back) * d) % NZ

    def attend(slot, g, masked):
        k = kv[pl.ds(pl.multiple_of(g * grp, grp), grp), :]
        v = kv[pl.ds(pl.multiple_of(vbase * sh + g * grp, grp), grp), :]
        if masked:
            q0 = home(slot) * sh
            k0 = ctx_of(x, g, y, 0) * sh
            qpos = q0 + lax.broadcasted_iota(jnp.int32, (sh, D), 0)
            lo = jnp.zeros((sh, D), jnp.int32)
            for i in range(3):
                lo = jnp.where(qpos >= docs[i], docs[i], lo)
            lane = lax.broadcasted_iota(jnp.int32, (sh, D), 1)
        def scores(h, b):
            q = qbuf[slot, b * ROWS:(b + 1) * ROWS, h * D:(h + 1) * D]
            return lax.dot_general(q, k, (((1,), (1,)), ((), ())), preferred_element_type=jnp.float32)

        def mask(s, b):
            parts = [s[:, j * D:(j + 1) * D] for j in range(grp // D)]
            if masked:
                here = slice(b * ROWS, (b + 1) * ROWS)
                parts = [
                    jnp.where(
                        (lane[here] + (k0 + j * D) <= qpos[here]) & (lane[here] + (k0 + j * D) >= lo[here]), part, NEG
                    )
                    for j, part in enumerate(parts)
                ]
            return parts

        def soft(s, h, b):
            here = slice(b * ROWS, (b + 1) * ROWS)
            parts = mask(s, b)
            top = functools.reduce(jnp.maximum, parts)
            old = mx[slot, h, here]
            new = jnp.maximum(old, jnp.max(top, axis=1, keepdims=True))
            mx[slot, h, here] = new
            new2 = new * C2
            parts = [jnp.exp2(part * C2 - new2) for part in parts]
            p = jnp.concatenate([part.astype(jnp.bfloat16) for part in parts], axis=1)
            decay = jnp.exp2(old * C2 - new2)
            tot[slot, h, here] = tot[slot, h, here] * decay + functools.reduce(jnp.add, parts)
            return p, decay

        def gather(p, decay, h, b):
            here = slice(b * ROWS, (b + 1) * ROWS)
            pv = jnp.dot(p, v, preferred_element_type=jnp.float32)
            acc[slot, h, here] = acc[slot, h, here] * decay + pv

        todo = [(h, b) for h in range(H) for b in range(sh // ROWS)]
        s = scores(*todo[0])
        for at, (h, b) in enumerate(todo):
            ahead = scores(*todo[at + 1]) if at + 1 < len(todo) else None
            p, decay = soft(s, h, b)
            gather(p, decay, h, b)
            s = ahead

    def task(slot, g):
        sx = slot // 2
        if_own = (sx == 0) & (g <= z) & jnp.logical_not((x == 1) & (z >= half) & (g < half))
        if_one = (sx == 1) & ((x == 2) | ((x == 1) & (g >= half)) | ((x == 0) & low))
        if_two = (sx == 2) & (x == 1) & (g >= half)
        needed = if_own | if_one | if_two
        masked = ((sx == 0) & (g == z)) | (x == 0) | ((sx == 0) & (x == 1) & low)

        @pl.when(needed & masked)
        def _():
            attend(slot, g, True)

        @pl.when(needed & jnp.logical_not(masked))
        def _():
            attend(slot, g, False)

    eye = lax.broadcasted_iota(jnp.int32, (D, D), 0) == lax.broadcasted_iota(jnp.int32, (D, D), 1)

    def finish(slot):
        for h in range(H):
            weight = jnp.broadcast_to(jnp.sum(tot[slot, h], axis=1, keepdims=True), (sh, D))
            osend[slot - 1, :, h * D:(h + 1) * D] = (acc[slot, h] / weight).astype(jnp.bfloat16)
            lse = mx[slot, h] * C2 + jnp.log2(weight)
            for b in range(sh // D):
                block = jnp.where(eye, lse[b * D:(b + 1) * D], 0.0)
                ssend[slot - 1, pl.ds(h * (sh // D) + b, 1), :] = jnp.sum(block, axis=0, keepdims=True)

    def o_copies(slot):
        to = home(slot)
        i = slot - 1
        return (
            send(osend.at[i], orecv.at[i], osent.at[i], osem.at[i], to),
            send(ssend.at[i], srecv.at[i], rsent.at[i], rsem.at[i], to),
        )

    @pl.loop(1, half + 2)
    def _(s):
        up_j = shard((z + NZ - s) % NZ, c)
        down_j = shard((z + s) % NZ, c)

        @pl.loop(0, pieces)
        def _(ch):
            late = ch // CUT
            last_up = half - late
            last_down = half - 1 + late

            @pl.when(s <= last_up)
            def _():
                kv_wait(up_j, ch)

                @pl.when(s < last_up)
                def _():
                    kv_send(up_j, ch, up)

            @pl.when(s <= last_down)
            def _():
                kv_wait(down_j, ch)

                @pl.when(s < last_down)
                def _():
                    kv_send(down_j, ch, down)

            @pl.when(s <= last_up)
            def _():
                kv_send(up_j, ch, twin)

            @pl.when(s <= last_down)
            def _():
                kv_send(down_j, ch, twin)

            n = 2 * s - 3 + ch // CUT

            @pl.when((n >= 0) & (n < NZ))
            def _():
                @pl.when(ch % CUT == 0)
                def _():
                    for part in range(pieces):
                        kv_wait(shard(group(n), 1 - c), part)

                @pl.loop(0, SLOTS // CUT)
                def _(t):
                    last = (n == NZ - 1).astype(jnp.int32)
                    slot = SLOTS - 1 - last * (SLOTS // CUT * (ch % CUT) + t) - (1 - last) * (ch % CUT + CUT * t)
                    begin = jnp.array(BEGIN[0], jnp.int32)
                    for at in range(1, SLOTS):
                        begin = jnp.where(slot == at, BEGIN[at], begin)
                    begin = jnp.where((x == NX - 1) & (slot == 1), 3, begin)

                    @pl.when(hosted(slot) & (n >= begin))
                    def _():
                        @pl.when((slot > 0) & (n == begin))
                        def _():
                            q_copy(slot).wait_recv()

                        start = n * (n > begin).astype(jnp.int32)

                        @pl.loop(start, n + 1)
                        def _(k):
                            task(slot, group(k))

                        early = ((x == 1) & (z >= half) & (slot > 1)).astype(jnp.int32)

                        @pl.when((n == NZ - 1 - early) & (slot > 0))
                        def _():
                            finish(slot)
                            for copy in o_copies(slot):
                                copy.start()

    def fold(slot):
        for copy in o_copies(slot):
            copy.wait_recv()
        for h in range(H):
            for b in range(sh // D):
                here = slice(b * D, (b + 1) * D)
                row = srecv[slot - 1, pl.ds(h * (sh // D) + b, 1), :]
                lse = jnp.broadcast_to(jnp.sum(jnp.where(eye, row, 0.0), axis=1, keepdims=True), (D, D))
                m2 = mx[0, h, here]
                best = jnp.maximum(m2, lse)
                keep = jnp.exp2(m2 - best)
                w = jnp.exp2(lse - best)
                part = orecv[slot - 1, here, h * D:(h + 1) * D].astype(jnp.float32)
                acc[0, h, here] = acc[0, h, here] * keep + part * w
                tot[0, h, here] = tot[0, h, here] * keep + w
                mx[0, h, here] = best

    for h in range(H):
        mx[0, h] = mx[0, h] * C2
        tot[0, h] = jnp.broadcast_to(jnp.sum(tot[0, h], axis=1, keepdims=True), (sh, D))

    @pl.loop(0, SLOTS - 2)
    def _(t):
        slot = 2 + (t + 2) % 4

        @pl.when(((slot < 4) & guest[1]) | ((slot >= 4) & guest[2]))
        def _():
            fold(slot)

    fold(1)
    for h in range(H):
        out[:, h * D:(h + 1) * D] = (acc[0, h] / tot[0, h]).astype(out.dtype)

    for slot in range(1, SLOTS):
        @pl.when(guest[slot // 2])
        def _(slot=slot):
            q_copy(slot).wait_send()

    for slot in range(1, SLOTS):
        @pl.when(host[slot // 2])
        def _(slot=slot):
            for copy in o_copies(slot):
                copy.wait_send()
    for ch in range(pieces):
        for i in range(2):
            first(ch, i).wait_send()
    send(kv.at[pl.ds(0, SENDS * sh)], kv.at[pl.ds(0, SENDS * sh)], kvsent, kvsem.at[0], twin).wait_send()


def shards(queries, keys, values, doc_starts):
    sh = keys.shape[0]
    any_spec = pl.BlockSpec(memory_space=pl.ANY)
    dma = pltpu.SemaphoreType.DMA
    return pl.pallas_call(
        kernel,
        out_shape=jax.ShapeDtypeStruct((sh, H * D), jnp.bfloat16),
        in_specs=[pl.BlockSpec(memory_space=pltpu.SMEM), any_spec, any_spec, any_spec],
        out_specs=pl.BlockSpec(memory_space=pltpu.VMEM),
        scratch_shapes=[
            pltpu.VMEM((SLOTS, sh, H * D), jnp.bfloat16),
            pltpu.VMEM((2 * NZ * NC * sh, D), jnp.bfloat16),
            pltpu.VMEM((SLOTS, H, sh, D), jnp.float32),
            pltpu.VMEM((SLOTS, H, sh, D), jnp.float32),
            pltpu.VMEM((SLOTS, H, sh, D), jnp.float32),
            pltpu.VMEM((SLOTS - 1, sh, H * D), jnp.bfloat16),
            pltpu.VMEM((SLOTS - 1, H * sh // D, D), jnp.float32),
            pltpu.VMEM((SLOTS - 1, sh, H * D), jnp.bfloat16),
            pltpu.VMEM((SLOTS - 1, H * sh // D, D), jnp.float32),
            dma((2 * CUT * NZ * NC,)), dma((SLOTS,)), dma((SLOTS - 1,)), dma((SLOTS - 1,)),
            dma, dma((4 * CUT,)), dma((SLOTS,)), dma((SLOTS - 1,)), dma((SLOTS - 1,)),
        ],
        compiler_params=pltpu.CompilerParams(collective_id=0, has_side_effects=True),
        name="ring_attention",
    )(doc_starts, queries, keys, values)


def solution(mesh):
    in_specs = (P("ctx", "head"), P("ctx", "head"), P("ctx", "head"), P("head"))
    out_specs = P("ctx", "head")
    return jax.shard_map(shards, mesh=mesh, in_specs=in_specs, out_specs=out_specs, check_vma=False)
```
